32 devices in a mesh: dp: 8 (over y, x, core), mp: 4 (over z).
Axes of the slice: x: 2, y: 2, z: 4, core: 2. Of those that a mesh axis runs over, the one named last changes fastest.
Arguments:
- features: bfloat16 [9216, 7168], P(('dp', 'mp')), may hold values from -6 to 6
- online_head: bfloat16 [7168, 128], P('dp'), may hold values from -0.0625 to 0.0625
- target_head: bfloat16 [7168, 128], P('dp'), may hold values from -0.0625 to 0.0625
- action_bin: int32 [9216], P(('dp', 'mp')), may hold values from 0 to 127
- next_index: int32 [9216], P(('dp', 'mp')), may hold values from 0 to 9215, as said below
- reward: float32 [9216], P(('dp', 'mp')), may hold values from 0 to 1
- terminal: int32 [9216], P(('dp', 'mp')), may hold values 0 or 1
Outputs:
- td_error: float32 [9216], P(('dp', 'mp'))
- head_grad: float32 [7168, 128], P('dp')
The draws below stay inside these ranges and needn't reach their ends.
Inputs may be any that keep to these rules, and one draw needn't show every extreme that they name: Where t mod 8 < 7, next_index[t] = t + 1; otherwise next_index[t] is a multiple of 8 inside the same aligned block of 1152 tokens as t.
All inputs are finite; a program needn't handle non-finite values. No bound on the sum of `terminal` on one device may be relied on, other than what follows from the above.
Results may differ from the reference program's by a relative error of at most 0.0029.
Values may be sent and summed in bfloat16 or wider, within the bound.
No kernel may reach another device: no remote copies, remote signals or barrier semaphores. Data moves between devices by JAX's collectives and lax.ppermute only.
A program may use at most 64 MiB of HBM per device.

```python
import math
import jax
import jax.numpy as jnp
from jax import lax

D = 7168
NB = 128
ADIM = 8
GROUP = 1152
TOKENS = 9216
N_DP = 8


def draw_next_index(key, part):
    position = jnp.arange(TOKENS, dtype=jnp.int32)
    group_start = position // GROUP * GROUP
    chosen = jax.random.randint(key, (TOKENS,), 0, GROUP // ADIM, dtype=jnp.int32)
    chosen = jnp.where(position == ADIM - 1, 0, chosen)
    jump_target = group_start + chosen * ADIM
    following = jnp.minimum(position + 1, TOKENS - 1)
    return jnp.where(position % ADIM == ADIM - 1, jump_target, following).astype(jnp.int32)


def place_ends(values, key, least, largest):
    shape = values.shape
    index_at = [jax.random.randint(jax.random.fold_in(key, axis), (), 0, shape[axis]) for axis in range(len(shape))]
    values = values.at[tuple(index_at)].set(least)
    longest = shape.index(max(shape))
    index_at[longest] = (index_at[longest] + 1) % shape[longest]
    return values.at[tuple(index_at)].set(largest)


def strengthened(result, rng, source, target, shards_of, factor):
    owner, partner = [(jnp.arange(result.shape[dim]) // (result.shape[dim] // shards_of)).reshape([-1 if axis == dim else 1 for axis in range(result.ndim)]) for dim in (source, target)]
    chosen = jax.random.permutation(rng, shards_of)[partner]
    strong = (owner == chosen) | (owner == (partner + shards_of // 2) % shards_of)
    return jnp.where(strong, factor * result, result)


def block_levels(key, shape, split, least, largest):
    factor_of, own = 1.0, jax.random.fold_in(key, 6)
    for axis_at, parts in split:
        draws = jnp.exp(jax.random.uniform(jax.random.fold_in(own, axis_at), (parts,), jnp.float32, least / len(split), largest / len(split)))
        factor_of = factor_of * jnp.repeat(draws, shape[axis_at] // parts).reshape([-1 if axis == axis_at else 1 for axis in range(len(shape))])
    return factor_of


def noise(rng, shape, deviation, reach, pieces=(), kind=jnp.bfloat16):
    values = jax.random.normal(rng, shape, jnp.float32) * deviation
    if len(pieces) > 0:
        values = block_levels(rng, shape, pieces, -0.22, 0.18) * values
    return jnp.clip(values, min=-reach, max=reach).astype(kind)


def gaussian_with(stream_key, extent, deviation, most, cuts, heavy, kind=jnp.bfloat16):
    array = deviation * jax.random.normal(stream_key, extent, jnp.float32)
    if cuts:
        array = array * block_levels(stream_key, extent, cuts, -0.22, 0.18)
    return jnp.clip(strengthened(array, jax.random.fold_in(stream_key, 3), *heavy), -most, most).astype(kind)


def setup_inputs(seed: int = 0) -> dict:
    keys = jax.random.split(jax.random.key(seed), 8)
    features = gaussian_with(keys[0], (TOKENS, D), 1.0, 6.0, ((0, 32),), (0, 1, 32, 2.75))
    online_head = noise(keys[1], (D, NB), D ** -0.5, 0.0625, ((0, 8),))
    target_head = noise(keys[2], (D, NB), D ** -0.5, 0.0625, ((0, 8),))
    action_bin = place_ends(jax.random.randint(keys[3], (TOKENS,), 0, NB), jax.random.fold_in(keys[3], 1), 0, NB - 1).astype(jnp.int32)
    next_index = draw_next_index(jax.random.fold_in(keys[7], 71), 0)
    reward = jnp.clip(1.0 * jax.random.uniform(keys[5], (TOKENS,), jnp.float32) ** block_levels(keys[5], (TOKENS,), ((0, 32),), -0.2, 0.2), 0.0, 1.0)
    terminal = place_ends((jax.random.randint(keys[6], (TOKENS,), 0, 4) < 1).astype(jnp.int32), jax.random.fold_in(keys[6], 1), 0, 1)
    return dict(features=features, online_head=online_head, target_head=target_head, action_bin=action_bin, next_index=next_index, reward=reward, terminal=terminal)


DISCOUNT = 0.98
CONSERVATIVE = 2.0

def reference(features, online_head, target_head, action_bin, next_index, reward, terminal):
    token_blocks = features.reshape(N_DP, GROUP, D)

    def best_of(token_block):
        logits = jnp.dot(token_block, target_head, preferred_element_type=jnp.float32)
        return lax.optimization_barrier(jnp.max(logits, axis=1))
    best_value = lax.map(best_of, token_blocks).reshape(TOKENS)
    next_best = jnp.take(best_value, next_index.astype(jnp.int32), axis=0)
    step_dim = jnp.arange(TOKENS, dtype=jnp.int32) % ADIM
    is_last = step_dim == ADIM - 1
    bootstrap = reward + DISCOUNT * (1.0 - terminal.astype(jnp.float32)) * next_best
    target_value = jnp.where(is_last, bootstrap, next_best)
    grad_scale = 1.0 / math.sqrt(TOKENS)

    def grad_block(running, scan_items):
        token_block, bins_taken, goal_value = scan_items
        q_values = jnp.dot(token_block, online_head, preferred_element_type=jnp.float32)
        onehot = (jnp.arange(NB, dtype=jnp.int32)[None, :] == bins_taken[:, None]).astype(jnp.float32)
        td_error = lax.optimization_barrier(jnp.sum(q_values * onehot, axis=1)) - goal_value
        q_grad = (grad_scale * (onehot * td_error[:, None] + (1.0 - onehot) * (CONSERVATIVE / (NB - 1)) * q_values)).astype(jnp.bfloat16)
        running = running + lax.dot_general(token_block, q_grad, (((0,), (0,)), ((), ())), preferred_element_type=jnp.float32)
        return (running, td_error)
    zero_grad = jnp.zeros((D, NB), jnp.float32)
    head_grad, td_error = lax.scan(grad_block, zero_grad, (token_blocks, action_bin.reshape(N_DP, GROUP), target_value.reshape(N_DP, GROUP)))
    return (td_error.reshape(TOKENS), head_grad)
```

```python
import math

import jax
import jax.numpy as jnp
from jax import lax
from jax.sharding import PartitionSpec as P

ADIM = 8


DISCOUNT = 0.98
CONSERVATIVE = 2.0


def across(value, mask):
    count = lax.axis_size("dp")
    return lax.ppermute(value, "dp", [(i, i ^ mask) for i in range(count)])


def shifted(value, step):
    count = lax.axis_size("mp")
    return lax.ppermute(value, "mp", [(i, (i + step) % count) for i in range(count)])


def gathered(shard, chips):
    half = shard.shape[0] // 2
    held = {0: (shard,)}
    for offset in sorted(range(1, chips), key=lambda o: (bin(o).count("1"), o)):
        low = offset & -offset
        high = 1 << (offset.bit_length() - 1)
        if low == high:
            held[offset] = (across(shard, 2 * offset),)
        else:
            first, second = held[offset ^ high], held[offset ^ low]
            first = first[0] if len(first) == 2 else first[0][:half]
            second = second[1] if len(second) == 2 else second[0][half:]
            held[offset] = (across(first, 2 * high), across(second, 2 * low))
    return held


def partial_logits(columns, held):
    total = None
    for offset, pieces in held.items():
        at = 0
        for piece in pieces:
            part = jnp.dot(
                columns[offset][:, at : at + piece.shape[0]],
                piece,
                preferred_element_type=jnp.float32,
            )
            total = part if total is None else total + part
            at += piece.shape[0]
    return total


def body(features, online_head, target_head, action_bin, next_index, reward, terminal):
    tok_rows = features.shape[0]
    head_rows, bin_count = online_head.shape
    mp_size = lax.axis_size("mp")
    dp_size = lax.axis_size("dp")
    chips = dp_size // 2
    group_size = tok_rows * mp_size
    all_tokens = group_size * dp_size
    dp_at = lax.axis_index("dp")
    mp_at = lax.axis_index("mp")
    core, chip = dp_at % 2, dp_at // 2
    steps = tok_rows // ADIM

    def cut(offset, parity):
        owner = 2 * (chip ^ offset) + parity
        return lax.dynamic_slice(features, (0, owner * head_rows), (tok_rows, head_rows))

    sent = [cut(o, 1 - core) for o in range(chips)]
    theirs = [across(s, 1) for s in sent]
    mine = [cut(o, core) for o in range(chips)]
    local_next = next_index - dp_at * group_size
    scalars = jnp.stack(
        [
            action_bin.astype(jnp.float32),
            local_next.astype(jnp.float32),
            reward,
            terminal.astype(jnp.float32),
        ]
    )
    scalars = (scalars, across(scalars, 1))

    target_held = gathered(target_head, chips)
    online_held = gathered(online_head, chips)

    part = (partial_logits(mine, target_held), partial_logits(theirs, target_held))
    logits = (part[0] + across(part[1], 1), part[1] + across(part[0], 1))
    best = [jnp.max(l, axis=1) for l in logits]
    firsts = jnp.stack([b.reshape(steps, ADIM)[:, 0] for b in best])
    from_mp = [firsts] + [shifted(firsts, k) for k in range(1, mp_size)]
    token = jnp.arange(tok_rows, dtype=jnp.int32)
    is_last = token % ADIM == ADIM - 1

    part = (partial_logits(mine, online_held), partial_logits(theirs, online_held))
    values = (part[0] + across(part[1], 1), part[1] + across(part[0], 1))

    grad_scale = 1.0 / math.sqrt(all_tokens)
    errors, q_grads = [], []
    for side in range(2):
        action, nxt, rew, term = (scalars[side][i] for i in range(4))
        action, nxt = action.astype(jnp.int32), nxt.astype(jnp.int32)
        step_at = nxt // ADIM
        table = jnp.concatenate([f[side] for f in from_mp])
        label = jnp.concatenate(
            [(mp_at - k + mp_size) % mp_size * steps + jnp.arange(steps) for k in range(mp_size)]
        )
        jumped = jnp.sum(
            jnp.where(step_at[:, None] == label[None, :], table[None, :], 0.0), axis=1
        )
        following = jnp.concatenate([best[side][1:], best[side][:1]])
        bootstrap = rew + DISCOUNT * (1.0 - term) * jumped
        target_value = jnp.where(is_last, bootstrap, following)
        taken = jnp.arange(bin_count, dtype=jnp.int32)[None, :] == action[:, None]
        td_error = jnp.sum(jnp.where(taken, values[side], 0.0), axis=1) - target_value
        q_grad = grad_scale * jnp.where(
            taken, td_error[:, None], (CONSERVATIVE / (bin_count - 1)) * values[side]
        )
        errors.append(td_error)
        q_grads.append(q_grad.astype(jnp.bfloat16))

    def term_of(offset):
        return sum(
            lax.dot_general(
                cols[offset], grad, (((0,), (0,)), ((), ())), preferred_element_type=jnp.float32
            )
            for cols, grad in zip((mine, theirs), q_grads)
        )

    arrived = [
        across(term_of(o).astype(jnp.bfloat16), 2 * o) for o in range(chips - 1, 0, -1)
    ]
    owned = term_of(0)
    for a in arrived:
        owned = owned + a.astype(jnp.float32)

    if head_rows % (16 * mp_size):
        return errors[0], lax.psum(owned, "mp")
    rows = head_rows // mp_size

    def rows_of(k):
        return lax.dynamic_slice(owned, ((mp_at + k) % mp_size * rows, 0), (rows, bin_count))

    piece = rows_of(0)
    for k in range(1, mp_size):
        piece = piece + shifted(rows_of(k).astype(jnp.bfloat16), k).astype(jnp.float32)
    piece = piece.astype(jnp.bfloat16)
    head_grad = jnp.zeros((head_rows, bin_count), jnp.float32)
    for k in range(mp_size):
        got = shifted(piece, k) if k else piece
        at = (mp_at - k + mp_size) % mp_size * rows
        head_grad = lax.dynamic_update_slice(head_grad, got.astype(jnp.float32), (at, 0))
    return errors[0], head_grad


def solution(mesh):
    placed = (
        P(("dp", "mp"), None),
        P("dp", None),
        P("dp", None),
        P(("dp", "mp")),
        P(("dp", "mp")),
        P(("dp", "mp")),
        P(("dp", "mp")),
    )
    return jax.shard_map(
        body,
        mesh=mesh,
        in_specs=placed,
        out_specs=(P(("dp", "mp")), P("dp", None)),
        check_vma=False,
    )
```

```python
import functools
import math

import jax
import jax.numpy as jnp
from jax import lax
from jax.experimental import pallas as pl
from jax.experimental.pallas import tpu as pltpu
from jax.sharding import PartitionSpec as P


ADIM = 8
LANES = 128


DISCOUNT = 0.98
CONSERVATIVE = 2.0


f32, bf16 = jnp.float32, jnp.bfloat16
VMEM = pl.BlockSpec(memory_space=pltpu.VMEM)
ANY = pl.BlockSpec(memory_space=pl.ANY)
MIB = 1 << 20
SMEM = pl.BlockSpec(memory_space=pltpu.SMEM)


def across(value, mask):
    count = lax.axis_size("dp")
    return lax.ppermute(value, "dp", [(i, i ^ mask) for i in range(count)])


def shifted(value, step):
    count = lax.axis_size("mp")
    return lax.ppermute(value, "mp", [(i, (i + step) % count) for i in range(count)])


def call(kernel, outs, *args, smem=0, scratch=()):
    return pl.pallas_call(
        kernel,
        out_shape=outs,
        scratch_shapes=scratch,
        in_specs=[SMEM] * smem + [VMEM] * (len(args) - smem),
        out_specs=jax.tree.map(lambda _: VMEM, outs),
        compiler_params=pltpu.CompilerParams(vmem_limit_bytes=16 * MIB),
    )(*args[:smem], *(kept(a) for a in args[smem:]))


def kept(value):
    return pltpu.with_memory_space_constraint(value, pltpu.VMEM)


def shape(*dims, dtype=f32):
    return pltpu.VMEM(dims, dtype)


def relay_order(chips):
    return sorted(range(1, chips), key=lambda o: (bin(o).count("1"), o))


def direct_hops(shard, chips):
    return {0: (shard,), **{o: (across(shard, 2 * o),) for o in relay_order(chips)}}


def first_hops(shard, chips):
    return {o: (across(shard, 2 * o),) for o in relay_order(chips) if o & (o - 1) == 0}


def halves_kernel(*refs):
    count = len(refs) // 3
    for ref, first_ref, second_ref in zip(refs[:count], refs[count::2], refs[count + 1 :: 2]):
        half = first_ref.shape[0]
        first_ref[...] = ref[:half]
        second_ref[...] = ref[half:]


def relayed(shard, held, chips):
    half = shape(shard.shape[0] // 2, shard.shape[1], dtype=shard.dtype)
    hops = [h[0] for h in held.values()]
    parts = call(halves_kernel, (half,) * (2 * len(hops)), *hops)
    split = dict(zip(held, zip(parts[::2], parts[1::2])))
    held = {0: (shard,), **held}
    for offset in relay_order(chips):
        if offset in held:
            continue
        low = offset & -offset
        high = 1 << (offset.bit_length() - 1)
        first = split.get(offset ^ high, held[offset ^ high])[0]
        second = split.get(offset ^ low, held[offset ^ low])[1]
        held[offset] = (across(first, 2 * high), across(second, 2 * low))
    return held


def column(ref, at_ref, offset, width):
    return ref.at[:, pl.ds(pl.multiple_of(at_ref[offset] * width, width), width)]


def cut_kernel(at_ref, features_ref, sent_ref):
    chips, _, width = sent_ref.shape
    for j in range(chips):
        sent_ref[j] = column(features_ref, at_ref, chips + j, width)[...]


def turn_kernel(at_ref, features_ref, theirs_ref, out_ref):
    for j in range(theirs_ref.shape[0]):
        mine = column(features_ref, at_ref, j, theirs_ref.shape[2])[...]
        both = jnp.concatenate([mine, theirs_ref[j]], axis=0)
        out_ref[j] = both.T


def logits_kernel(offsets, has_start, at_ref, features_ref, theirs_ref, *refs):
    pieces, out_ref = refs[: len(offsets)], refs[-1]
    width = theirs_ref.shape[2]
    for side in range(2):
        total = refs[-2][side] if has_start else None
        for (offset, at), piece in zip(offsets, pieces):
            cols = (theirs_ref.at[offset], column(features_ref, at_ref, offset, width))[1 - side]
            part = jnp.dot(
                cols[:, at : at + piece.shape[0]], piece[...], preferred_element_type=f32
            )
            total = part if total is None else total + part
        out_ref[side] = total


def partial_logits(at, features, theirs, held, start=None):
    offsets, pieces = [], []
    for offset, parts in held.items():
        row = 0
        for part in parts:
            offsets.append((offset, row))
            pieces.append(part)
            row += part.shape[0]
    out = shape(2, features.shape[0], pieces[0].shape[1])
    extra = () if start is None else (start,)
    kernel = functools.partial(logits_kernel, tuple(offsets), start is not None)
    return call(kernel, out, at, features, theirs, *pieces, *extra, smem=1)


def best_kernel(part_ref, other_ref, best_ref, firsts_ref):
    tokens = part_ref.shape[1]
    lanes = firsts_ref.shape[1]
    token = lax.broadcasted_iota(jnp.int32, (tokens, lanes), 0)
    lane = lax.broadcasted_iota(jnp.int32, (tokens, lanes), 1)
    for side in range(2):
        best = jnp.max(part_ref[side] + other_ref[1 - side], axis=1, keepdims=True)
        best_ref[side] = jnp.broadcast_to(best, best_ref.shape[1:])
        picked = jnp.where(token == ADIM * lane, best, 0.0)
        firsts_ref[side : side + 1] = jnp.sum(picked, axis=0, keepdims=True)


def goal_kernel(sources_at, at_ref, best_ref, scalar_ref, other_ref, *refs):
    *firsts, out_ref, rows_ref = refs
    tokens = best_ref.shape[1]
    lanes = firsts[0].shape[1]
    steps = tokens // ADIM
    rows_ref[...] = jnp.zeros_like(rows_ref)
    rows_ref[:4, :tokens] = scalar_ref[...]
    rows_ref[4:, :tokens] = other_ref[...]
    columns = rows_ref[...].T
    lane = lax.broadcasted_iota(jnp.int32, (tokens, lanes), 1)
    token = lax.broadcasted_iota(jnp.int32, (tokens, 1), 0)
    is_last = (token & (ADIM - 1)) == ADIM - 1
    for side in range(2):
        action, nxt, rew, term = (
            columns[:tokens, 4 * side + i : 4 * side + i + 1] for i in range(4)
        )
        step_at = nxt.astype(jnp.int32) >> (ADIM.bit_length() - 1)
        jumped = jnp.zeros((tokens, lanes), f32)
        for k, table in enumerate(firsts):
            label = lane + at_ref[sources_at + k] * steps
            hit = (label == step_at) & (lane < steps)
            jumped = jnp.where(hit, table[side : side + 1], jumped)
        jumped = jnp.sum(jumped, axis=1, keepdims=True)
        following = pltpu.roll(best_ref[side], tokens - 1, 0)[:, :1]
        bootstrap = rew + DISCOUNT * (1.0 - term) * jumped
        goal = jnp.where(is_last, bootstrap, following)
        first = lax.broadcasted_iota(jnp.int32, (tokens, LANES), 1) == 0
        out_ref[side] = jnp.where(first, goal, action)


def grad_kernel(grad_scale, at, part_ref, other_ref, goal_ref, cols_ref, grad_ref, error_ref, out_ref):
    tokens, bins = part_ref.shape[1:]
    lane = lax.broadcasted_iota(jnp.int32, (tokens, bins), 1)
    for side in range(2):
        values = part_ref[side] + other_ref[1 - side]
        goal = goal_ref[side]
        taken = lane == goal[:, 1:2].astype(jnp.int32)
        td_error = jnp.sum(jnp.where(taken, values, 0.0), axis=1, keepdims=True) - goal[:, :1]
        grad = grad_scale * jnp.where(taken, td_error, (CONSERVATIVE / (bins - 1)) * values)
        grad_ref[side * tokens : (side + 1) * tokens] = grad.astype(bf16)
        if side == 0:
            error_ref[...] = jnp.broadcast_to(td_error, error_ref.shape)
    out_ref[...] = jnp.dot(cols_ref[at], grad_ref[...], preferred_element_type=f32).astype(
        out_ref.dtype
    )


def term_kernel(offsets, cols_ref, grad_ref, *outs):
    for offset, out_ref in zip(offsets, outs):
        out_ref[...] = jnp.dot(
            cols_ref[offset], grad_ref[...], preferred_element_type=f32
        ).astype(out_ref.dtype)


def plain_body(features, online_head, target_head, action_bin, next_index, reward, terminal):
    tok_rows = features.shape[0]
    bin_count = online_head.shape[1]
    group_size = tok_rows * lax.axis_size("mp")
    all_tokens = group_size * lax.axis_size("dp")
    online_full = lax.all_gather(online_head, "dp", axis=0, tiled=True)
    columns = features
    target_logits = jnp.dot(
        columns,
        lax.all_gather(target_head, "dp", axis=0, tiled=True),
        preferred_element_type=jnp.float32,
    )
    best_value = jnp.max(target_logits, axis=1)
    local_next = next_index - lax.axis_index("dp") * group_size
    step_dim = jnp.arange(tok_rows, dtype=jnp.int32) % ADIM
    is_last = step_dim == ADIM - 1
    group_best = lax.all_gather(best_value, "mp", axis=0, tiled=True)
    next_best = jnp.take(group_best, local_next, axis=0)
    bootstrap = reward + DISCOUNT * (1.0 - terminal.astype(jnp.float32)) * next_best
    target_value = jnp.where(is_last, bootstrap, next_best)
    q_values = jnp.dot(features, online_full, preferred_element_type=jnp.float32)
    onehot = (jnp.arange(bin_count, dtype=jnp.int32)[None, :] == action_bin[:, None]).astype(
        jnp.float32
    )
    td_error = jnp.sum(q_values * onehot, axis=1) - target_value
    grad_scale = 1.0 / math.sqrt(all_tokens)
    q_grad = (
        grad_scale
        * (
            onehot * td_error[:, None]
            + (1.0 - onehot) * (CONSERVATIVE / (bin_count - 1)) * q_values
        )
    ).astype(jnp.bfloat16)
    columns = features
    grad_owned = lax.psum_scatter(
        lax.dot_general(
            columns, q_grad, (((0,), (0,)), ((), ())), preferred_element_type=jnp.float32
        ),
        "dp",
        scatter_dimension=0,
        tiled=True,
    )
    head_grad = lax.psum(grad_owned, "mp")
    return (td_error, head_grad)


def body(features, online_head, target_head, action_bin, next_index, reward, terminal):
    tokens = features.shape[0]
    head_rows, bins = online_head.shape
    mp_size = lax.axis_size("mp")
    dp_size = lax.axis_size("dp")
    if head_rows % LANES or head_rows % (16 * mp_size) or dp_size & (dp_size - 1):
        return plain_body(
            features, online_head, target_head, action_bin, next_index, reward, terminal
        )
    chips = dp_size // 2
    group_size = tokens * mp_size
    all_tokens = group_size * dp_size
    dp_at = lax.axis_index("dp")
    mp_at = lax.axis_index("mp")
    core, chip = dp_at & 1, dp_at >> 1

    target_held = direct_hops(target_head, chips)
    online_hops = first_hops(online_head, chips)

    offset = jnp.arange(chips, dtype=jnp.int32)
    owner = 2 * (chip ^ offset)
    at, other_at = owner + core, owner + 1 - core
    sources = mp_at - jnp.arange(mp_size, dtype=jnp.int32)
    sources = jnp.where(sources < 0, sources + mp_size, sources)
    at = jnp.concatenate([at, other_at, sources])
    block = shape(chips, tokens, head_rows, dtype=features.dtype)
    sent = call(cut_kernel, block, at, features, smem=1)
    theirs = across(sent, 1)
    scalars = jnp.stack(
        [
            action_bin.astype(f32),
            (next_index - dp_at * group_size).astype(f32),
            reward,
            terminal.astype(f32),
        ]
    )
    scalars = (scalars, across(scalars, 1))
    out = shape(chips, head_rows, 2 * tokens, dtype=features.dtype)
    cols_turned = call(turn_kernel, out, at, features, theirs, smem=1)
    online_held = relayed(online_head, online_hops, chips)

    last = chips - 1
    both = shape(2, tokens, bins)

    def logits(held):
        early = {o: p for o, p in held.items() if o != last}
        part = partial_logits(at, features, theirs, early)
        part = partial_logits(at, features, theirs, {last: held[last]}, part)
        return part, across(part, 1)

    parts = logits(target_held)
    lanes = -(-(tokens // ADIM) // LANES) * LANES
    best, firsts = call(best_kernel, (both, shape(2, lanes)), *parts)
    tables = [firsts]
    for k in range(1, mp_size):
        tables.append(shifted(firsts, k))
    goal = call(
        functools.partial(goal_kernel, 2 * chips), both, at, best, *scalars, *tables, smem=1,
        scratch=[pltpu.VMEM((8, -(-tokens // LANES) * LANES), f32)],
    )

    parts = logits(online_held)
    grad_scale = 1.0 / math.sqrt(all_tokens)
    block = shape(head_rows, bins, dtype=bf16)
    q_grad, error, term = call(
        functools.partial(grad_kernel, grad_scale, last),
        (shape(2 * tokens, bins, dtype=bf16), shape(tokens, bins), block),
        *parts,
        goal,
        cols_turned,
    )
    arrived = [across(term, 2 * last)]
    rest = tuple(range(last - 1, 0, -1))
    *terms, owned = call(
        functools.partial(term_kernel, rest + (0,)),
        (*(block for _ in rest), shape(head_rows, bins)),
        cols_turned,
        q_grad,
    )
    arrived += [across(t, 2 * o) for o, t in zip(rest, terms)]
    for a in arrived:
        owned = owned + a.astype(f32)
    td_error = error[:, 0]

    rows = head_rows // mp_size

    def rows_of(k):
        return lax.dynamic_slice(owned, ((mp_at + k) % mp_size * rows, 0), (rows, bins))

    piece = rows_of(0)
    for k in range(1, mp_size):
        piece = piece + shifted(rows_of(k).astype(bf16), k).astype(f32)
    piece = piece.astype(bf16)
    head_grad = jnp.zeros((head_rows, bins), f32)
    for k in range(mp_size):
        got = shifted(piece, k) if k else piece
        at = (mp_at - k + mp_size) % mp_size * rows
        head_grad = lax.dynamic_update_slice(head_grad, got.astype(f32), (at, 0))
    return td_error, head_grad


def solution(mesh):
    placed = (
        P(("dp", "mp"), None),
        P("dp", None),
        P("dp", None),
        P(("dp", "mp")),
        P(("dp", "mp")),
        P(("dp", "mp")),
        P(("dp", "mp")),
    )


    return jax.shard_map(
        body,
        mesh=mesh,
        in_specs=placed,
        out_specs=(P(("dp", "mp")), P("dp", None)),
        check_vma=False,
    )
```

```python
import functools
import math

import jax
import jax.numpy as jnp
from jax import lax
from jax.experimental import pallas as pl
from jax.experimental.pallas import tpu as pltpu
from jax.sharding import PartitionSpec as P


ADIM = 8
LANES = 128


DISCOUNT = 0.98
CONSERVATIVE = 2.0


f32, bf16 = jnp.float32, jnp.bfloat16
VMEM = pl.BlockSpec(memory_space=pltpu.VMEM)
ANY = pl.BlockSpec(memory_space=pl.ANY)
MIB = 1 << 20
SMEM = pl.BlockSpec(memory_space=pltpu.SMEM)


def across(value, mask):
    count = lax.axis_size("dp")
    return lax.ppermute(value, "dp", [(i, i ^ mask) for i in range(count)])


def mixed(value, mask):
    count = lax.axis_size("mp")
    return lax.ppermute(value, "mp", [(i, i ^ mask) for i in range(count)])


def call(kernel, outs, *args, smem=0, scratch=()):
    return pl.pallas_call(
        kernel,
        out_shape=outs,
        scratch_shapes=scratch,
        in_specs=[SMEM] * smem + [VMEM] * (len(args) - smem),
        out_specs=jax.tree.map(lambda _: VMEM, outs),
        compiler_params=pltpu.CompilerParams(vmem_limit_bytes=16 * MIB),
    )(*args[:smem], *(kept(a) for a in args[smem:]))


def kept(value):
    return pltpu.with_memory_space_constraint(value, pltpu.VMEM)


def shape(*dims, dtype=f32):
    return pltpu.VMEM(dims, dtype)


def relay_order(chips):
    return sorted(range(1, chips), key=lambda o: (bin(o).count("1"), o))


def direct_hops(shard, chips):
    return {0: (shard,), **{o: (across(shard, 2 * o),) for o in relay_order(chips)}}


def column(ref, at_ref, offset, width):
    return ref.at[:, pl.ds(pl.multiple_of(at_ref[offset] * width, width), width)]


def load_kernel(features_ref, out_ref, sem):
    copy = pltpu.make_async_copy(features_ref, out_ref, sem)
    copy.start()
    copy.wait()


def loaded(features):
    return pl.pallas_call(
        load_kernel,
        out_shape=shape(*features.shape, dtype=features.dtype),
        in_specs=[ANY],
        out_specs=VMEM,
        scratch_shapes=[pltpu.SemaphoreType.DMA],
        compiler_params=pltpu.CompilerParams(vmem_limit_bytes=16 * MIB),
        name="load",
    )(pltpu.with_memory_space_constraint(features, pltpu.HBM))


def turn_kernel(at_ref, features_ref, theirs_ref, out_ref):
    chips, width, _ = out_ref.shape
    for j in range(chips):
        both = [column(ref, at_ref, j, width)[...] for ref in (features_ref, theirs_ref)]
        both = jnp.concatenate(both, axis=0)
        out_ref[j] = both.T


def logits_kernel(width, offsets, has_start, at_ref, features_ref, theirs_ref, *refs):
    pieces, out_ref = refs[: len(offsets)], refs[-1]
    for side, ref in enumerate((features_ref, theirs_ref)):
        total = refs[-2][side] if has_start else None
        for (offset, at), piece in zip(offsets, pieces):
            cols = column(ref, at_ref, offset, width)
            part = jnp.dot(
                cols[:, at : at + piece.shape[0]], piece[...], preferred_element_type=f32
            )
            total = part if total is None else total + part
        out_ref[side] = total


def partial_logits(width, at, features, theirs, held, start=None):
    offsets, pieces = [], []
    for offset, parts in held.items():
        row = 0
        for part in parts:
            offsets.append((offset, row))
            pieces.append(part)
            row += part.shape[0]
    out = shape(2, features.shape[0], pieces[0].shape[1])
    extra = () if start is None else (start,)
    kernel = functools.partial(logits_kernel, width, tuple(offsets), start is not None)
    return call(kernel, out, at, features, theirs, *pieces, *extra, smem=1)


def best_kernel(part_ref, other_ref, best_ref, firsts_ref):
    tokens = part_ref.shape[1]
    lanes = firsts_ref.shape[1]
    token = lax.broadcasted_iota(jnp.int32, (tokens, lanes), 0)
    lane = lax.broadcasted_iota(jnp.int32, (tokens, lanes), 1)
    for side in range(2):
        best = jnp.max(part_ref[side] + other_ref[1 - side], axis=1, keepdims=True)
        best_ref[side] = jnp.broadcast_to(best, best_ref.shape[1:])
        picked = jnp.where(token == ADIM * lane, best, 0.0)
        firsts_ref[side : side + 1] = jnp.sum(picked, axis=0, keepdims=True)


def join_kernel(first_ref, second_ref, out_ref):
    rows = first_ref.shape[0]
    out_ref[:rows] = first_ref[...]
    out_ref[rows:] = second_ref[...]


def goal_kernel(sources_at, at_ref, best_ref, scalar_ref, other_ref, *refs):
    *firsts, out_ref, rows_ref = refs
    tokens = best_ref.shape[1]
    lanes = firsts[0].shape[1]
    steps = tokens // ADIM
    rows_ref[...] = jnp.zeros_like(rows_ref)
    rows_ref[:4, :tokens] = scalar_ref[...]
    rows_ref[4:, :tokens] = other_ref[...]
    columns = rows_ref[...].T
    lane = lax.broadcasted_iota(jnp.int32, (tokens, lanes), 1)
    token = lax.broadcasted_iota(jnp.int32, (tokens, 1), 0)
    is_last = (token & (ADIM - 1)) == ADIM - 1
    for side in range(2):
        action, nxt, rew, term = (
            columns[:tokens, 4 * side + i : 4 * side + i + 1] for i in range(4)
        )
        local = nxt.astype(jnp.int32) - at_ref[at_ref.shape[0] - 2 + side]
        step_at = local >> (ADIM.bit_length() - 1)
        jumped = jnp.zeros((tokens, lanes), f32)
        tables = [t[i : i + 1] for t in firsts for i in range(side, t.shape[0], 2)]
        for k, table in enumerate(tables):
            label = lane + at_ref[sources_at + k] * steps
            hit = (label == step_at) & (lane < steps)
            jumped = jnp.where(hit, table, jumped)
        jumped = jnp.sum(jumped, axis=1, keepdims=True)
        following = pltpu.roll(best_ref[side], tokens - 1, 0)[:, :1]
        bootstrap = rew + DISCOUNT * (1.0 - term) * jumped
        goal = jnp.where(is_last, bootstrap, following)
        first = lax.broadcasted_iota(jnp.int32, (tokens, LANES), 1) == 0
        out_ref[side] = jnp.where(first, goal, action)


def grad_kernel(grad_scale, at, part_ref, other_ref, goal_ref, cols_ref, grad_ref, error_ref, out_ref):
    tokens, bins = part_ref.shape[1:]
    lane = lax.broadcasted_iota(jnp.int32, (tokens, bins), 1)
    for side in range(2):
        values = part_ref[side] + other_ref[1 - side]
        goal = goal_ref[side]
        taken = lane == goal[:, 1:2].astype(jnp.int32)
        td_error = jnp.sum(jnp.where(taken, values, 0.0), axis=1, keepdims=True) - goal[:, :1]
        grad = grad_scale * jnp.where(taken, td_error, (CONSERVATIVE / (bins - 1)) * values)
        grad_ref[side * tokens : (side + 1) * tokens] = grad.astype(bf16)
        if side == 0:
            error_ref[...] = jnp.broadcast_to(td_error, error_ref.shape)
    out_ref[...] = jnp.dot(cols_ref[at], grad_ref[...], preferred_element_type=f32).astype(
        out_ref.dtype
    )


def term_kernel(offsets, cols_ref, grad_ref, *outs):
    for offset, out_ref in zip(offsets, outs):
        out_ref[...] = jnp.dot(
            cols_ref[offset], grad_ref[...], preferred_element_type=f32
        ).astype(out_ref.dtype)


def plain_body(features, online_head, target_head, action_bin, next_index, reward, terminal):
    tok_rows = features.shape[0]
    bin_count = online_head.shape[1]
    group_size = tok_rows * lax.axis_size("mp")
    all_tokens = group_size * lax.axis_size("dp")
    online_full = lax.all_gather(online_head, "dp", axis=0, tiled=True)
    columns = features
    target_logits = jnp.dot(
        columns,
        lax.all_gather(target_head, "dp", axis=0, tiled=True),
        preferred_element_type=jnp.float32,
    )
    best_value = jnp.max(target_logits, axis=1)
    local_next = next_index - lax.axis_index("dp") * group_size
    step_dim = jnp.arange(tok_rows, dtype=jnp.int32) % ADIM
    is_last = step_dim == ADIM - 1
    group_best = lax.all_gather(best_value, "mp", axis=0, tiled=True)
    next_best = jnp.take(group_best, local_next, axis=0)
    bootstrap = reward + DISCOUNT * (1.0 - terminal.astype(jnp.float32)) * next_best
    target_value = jnp.where(is_last, bootstrap, next_best)
    q_values = jnp.dot(features, online_full, preferred_element_type=jnp.float32)
    onehot = (jnp.arange(bin_count, dtype=jnp.int32)[None, :] == action_bin[:, None]).astype(
        jnp.float32
    )
    td_error = jnp.sum(q_values * onehot, axis=1) - target_value
    grad_scale = 1.0 / math.sqrt(all_tokens)
    q_grad = (
        grad_scale
        * (
            onehot * td_error[:, None]
            + (1.0 - onehot) * (CONSERVATIVE / (bin_count - 1)) * q_values
        )
    ).astype(jnp.bfloat16)
    columns = features
    grad_owned = lax.psum_scatter(
        lax.dot_general(
            columns, q_grad, (((0,), (0,)), ((), ())), preferred_element_type=jnp.float32
        ),
        "dp",
        scatter_dimension=0,
        tiled=True,
    )
    head_grad = lax.psum(grad_owned, "mp")
    return (td_error, head_grad)


def body(features, online_head, target_head, action_bin, next_index, reward, terminal):
    tokens = features.shape[0]
    head_rows, bins = online_head.shape
    mp_size = lax.axis_size("mp")
    dp_size = lax.axis_size("dp")
    odd = dp_size & (dp_size - 1) or mp_size & (mp_size - 1)
    if odd or head_rows % LANES or head_rows % (16 * mp_size):
        return plain_body(
            features, online_head, target_head, action_bin, next_index, reward, terminal
        )
    chips = dp_size // 2
    group_size = tokens * mp_size
    all_tokens = group_size * dp_size
    dp_at = lax.axis_index("dp")
    mp_at = lax.axis_index("mp")
    core, chip = dp_at & 1, dp_at >> 1

    offset = jnp.arange(chips, dtype=jnp.int32)
    owner = 2 * (chip ^ offset) + core
    sources = mp_at ^ jnp.arange(mp_size, dtype=jnp.int32)
    groups = (dp_at ^ jnp.arange(2, dtype=jnp.int32)) * group_size
    at = jnp.concatenate([owner, sources, groups])
    target_held = direct_hops(target_head, chips)
    theirs = across(features, 1)
    online_held = direct_hops(online_head, chips)

    scalars = jnp.stack(
        [
            action_bin.astype(f32),
            next_index.astype(f32),
            reward,
            terminal.astype(f32),
        ]
    )
    scalars = (scalars, across(scalars, 1))
    features = loaded(features)
    out = shape(chips, head_rows, 2 * tokens, dtype=features.dtype)
    cols_turned = call(turn_kernel, out, at, features, theirs, smem=1)

    last = chips - 1
    both = shape(2, tokens, bins)

    def logits(held):
        early = {o: p for o, p in held.items() if o < chips // 2}
        late = {o: p for o, p in held.items() if o not in early}
        part = partial_logits(head_rows, at, features, theirs, early)
        part = partial_logits(head_rows, at, features, theirs, late, part)
        return part, across(part, 1)

    parts = logits(target_held)
    lanes = -(-(tokens // ADIM) // LANES) * LANES
    best, firsts = call(best_kernel, (both, shape(2, lanes)), *parts)
    tables, mask = [firsts], 1
    while mask < mp_size:
        if mask > 1:
            out = shape(2 * mask, lanes)
            tables = [call(join_kernel, out, *tables)]
        tables.append(mixed(tables[0], mask))
        mask *= 2
    goal = call(
        functools.partial(goal_kernel, chips), both, at, best, *scalars, *tables, smem=1,
        scratch=[pltpu.VMEM((8, -(-tokens // LANES) * LANES), f32)],
    )

    parts = logits(online_held)
    grad_scale = 1.0 / math.sqrt(all_tokens)
    block = shape(head_rows, bins, dtype=bf16)
    q_grad, error, term = call(
        functools.partial(grad_kernel, grad_scale, last),
        (shape(2 * tokens, bins, dtype=bf16), shape(tokens, bins), block),
        *parts,
        goal,
        cols_turned,
    )
    arrived = [across(term, 2 * last)]
    rest = tuple(range(last - 1, 0, -1))
    *terms, owned = call(
        functools.partial(term_kernel, rest + (0,)),
        (*(block for _ in rest), shape(head_rows, bins)),
        cols_turned,
        q_grad,
    )
    arrived += [across(t, 2 * o) for o, t in zip(rest, terms)]
    for a in arrived:
        owned = owned + a.astype(f32)
    td_error = error[:, 0]

    rows = head_rows // mp_size

    def rows_of(k):
        return lax.dynamic_slice(owned, ((mp_at ^ k) * rows, 0), (rows, bins))

    order = sorted(range(1, mp_size), key=lambda k: -(k >> 1))
    piece = rows_of(0)
    for k in order:
        got = mixed(rows_of(k).astype(bf16), k)
        piece = piece + got.astype(f32)
    piece = piece.astype(bf16)
    head_grad = jnp.zeros((head_rows, bins), f32)
    for k in [0] + order:
        got = mixed(piece, k) if k else piece
        head_grad = lax.dynamic_update_slice(head_grad, got.astype(f32), ((mp_at ^ k) * rows, 0))
    return td_error, head_grad


def solution(mesh):
    placed = (
        P(("dp", "mp"), None),
        P("dp", None),
        P("dp", None),
        P(("dp", "mp")),
        P(("dp", "mp")),
        P(("dp", "mp")),
        P(("dp", "mp")),
    )


    return jax.shard_map(
        body,
        mesh=mesh,
        in_specs=placed,
        out_specs=(P(("dp", "mp")), P("dp", None)),
        check_vma=False,
    )
```

```python
import functools
import math

import jax
import jax.numpy as jnp
from jax import lax
from jax.experimental import pallas as pl
from jax.experimental.pallas import tpu as pltpu
from jax.sharding import PartitionSpec as P


ADIM = 8
LANES = 128


DISCOUNT = 0.98
CONSERVATIVE = 2.0


f32, bf16 = jnp.float32, jnp.bfloat16
VMEM = pl.BlockSpec(memory_space=pltpu.VMEM)
ANY = pl.BlockSpec(memory_space=pl.ANY)
MIB = 1 << 20
SMEM = pl.BlockSpec(memory_space=pltpu.SMEM)


def across(value, mask):
    count = lax.axis_size("dp")
    return lax.ppermute(value, "dp", [(i, i ^ mask) for i in range(count)])


def mixed(value, mask):
    count = lax.axis_size("mp")
    return lax.ppermute(value, "mp", [(i, i ^ mask) for i in range(count)])


def call(kernel, outs, *args, smem=0, scratch=()):
    return pl.pallas_call(
        kernel,
        out_shape=outs,
        scratch_shapes=scratch,
        in_specs=[SMEM] * smem + [VMEM] * (len(args) - smem),
        out_specs=jax.tree.map(lambda _: VMEM, outs),
        compiler_params=pltpu.CompilerParams(vmem_limit_bytes=16 * MIB),
    )(*args[:smem], *(kept(a) for a in args[smem:]))


def kept(value):
    return pltpu.with_memory_space_constraint(value, pltpu.VMEM)


def shape(*dims, dtype=f32):
    return pltpu.VMEM(dims, dtype)


def direct_hops(shard, chips):
    held = {0: (shard,)}
    for offset in range(1, chips):
        held[offset] = (across(shard, 2 * offset),)
    return held


def column(ref, at_ref, offset, width):
    return ref.at[:, pl.ds(pl.multiple_of(at_ref[offset] * width, width), width)]


def turn_kernel(at_ref, features_ref, theirs_ref, kept_ref, out_ref, sems):
    chips, width, _ = out_ref.shape
    columns = [(column(features_ref, at_ref, j, width), column(kept_ref, at_ref, j, width)) for j in range(chips)]
    copies = [pltpu.make_async_copy(*pair, sems.at[j]) for j, pair in enumerate(columns)]
    for copy in copies:
        copy.start()
    for j, copy in enumerate(copies):
        copy.wait()
        both = [column(ref, at_ref, j, width)[...] for ref in (kept_ref, theirs_ref)]
        out_ref[j] = jnp.concatenate(both, axis=0).T


def turned(at, features, theirs, chips, width):
    rows = features.shape[0]
    return pl.pallas_call(
        turn_kernel,
        out_shape=(
            shape(*features.shape, dtype=features.dtype),
            shape(chips, width, 2 * rows, dtype=features.dtype),
        ),
        in_specs=[SMEM, ANY, VMEM],
        out_specs=(VMEM, VMEM),
        scratch_shapes=[pltpu.SemaphoreType.DMA((chips,))],
        compiler_params=pltpu.CompilerParams(vmem_limit_bytes=16 * MIB),
        name="turn_columns",
    )(at, pltpu.with_memory_space_constraint(features, pltpu.HBM), kept(theirs))


def logits_kernel(width, offsets, has_start, at_ref, features_ref, theirs_ref, *refs):
    pieces, out_ref = refs[: len(offsets)], refs[-1]
    for side, ref in enumerate((features_ref, theirs_ref)):
        total = refs[-2][side] if has_start else None
        for (offset, at), piece in zip(offsets, pieces):
            cols = column(ref, at_ref, offset, width)
            part = jnp.dot(
                cols[:, at : at + piece.shape[0]], piece[...], preferred_element_type=f32
            )
            total = part if total is None else total + part
        out_ref[side] = total


def partial_logits(width, at, features, theirs, held, start=None):
    offsets, pieces = [], []
    for offset, parts in held.items():
        row = 0
        for part in parts:
            offsets.append((offset, row))
            pieces.append(part)
            row += part.shape[0]
    out = shape(2, features.shape[0], pieces[0].shape[1])
    extra = () if start is None else (start,)
    kernel = functools.partial(logits_kernel, width, tuple(offsets), start is not None)
    return call(kernel, out, at, features, theirs, *pieces, *extra, smem=1)


def best_kernel(part_ref, other_ref, best_ref, firsts_ref):
    tokens = part_ref.shape[1]
    lanes = firsts_ref.shape[1]
    token = lax.broadcasted_iota(jnp.int32, (tokens, lanes), 0)
    lane = lax.broadcasted_iota(jnp.int32, (tokens, lanes), 1)
    for side in range(2):
        best = jnp.max(part_ref[side] + other_ref[1 - side], axis=1, keepdims=True)
        best_ref[side] = jnp.broadcast_to(best, best_ref.shape[1:])
        picked = jnp.where(token == ADIM * lane, best, 0.0)
        firsts_ref[side : side + 1] = jnp.sum(picked, axis=0, keepdims=True)


def join_kernel(first_ref, second_ref, out_ref):
    rows = first_ref.shape[0]
    out_ref[:rows] = first_ref[...]
    out_ref[rows:] = second_ref[...]


def goal_kernel(sources_at, at_ref, best_ref, scalar_ref, other_ref, *refs):
    *firsts, out_ref, rows_ref = refs
    tokens = best_ref.shape[1]
    lanes = firsts[0].shape[1]
    steps = tokens // ADIM
    rows_ref[...] = jnp.zeros_like(rows_ref)
    rows_ref[:4, :tokens] = scalar_ref[...]
    rows_ref[4:, :tokens] = other_ref[...]
    columns = rows_ref[...].T
    lane = lax.broadcasted_iota(jnp.int32, (tokens, lanes), 1)
    token = lax.broadcasted_iota(jnp.int32, (tokens, 1), 0)
    is_last = (token & (ADIM - 1)) == ADIM - 1
    for side in range(2):
        action, nxt, rew, term = (
            columns[:tokens, 4 * side + i : 4 * side + i + 1] for i in range(4)
        )
        local = nxt.astype(jnp.int32) - at_ref[at_ref.shape[0] - 2 + side]
        step_at = local >> (ADIM.bit_length() - 1)
        jumped = jnp.zeros((tokens, lanes), f32)
        tables = [t[i : i + 1] for t in firsts for i in range(side, t.shape[0], 2)]
        for k, table in enumerate(tables):
            label = lane + at_ref[sources_at + k] * steps
            hit = (label == step_at) & (lane < steps)
            jumped = jnp.where(hit, table, jumped)
        jumped = jnp.sum(jumped, axis=1, keepdims=True)
        following = pltpu.roll(best_ref[side], tokens - 1, 0)[:, :1]
        bootstrap = rew + DISCOUNT * (1.0 - term) * jumped
        goal = jnp.where(is_last, bootstrap, following)
        first = lax.broadcasted_iota(jnp.int32, (tokens, LANES), 1) == 0
        out_ref[side] = jnp.where(first, goal, action)


def grad_kernel(grad_scale, at, part_ref, other_ref, goal_ref, cols_ref, grad_ref, error_ref, out_ref):
    tokens, bins = part_ref.shape[1:]
    lane = lax.broadcasted_iota(jnp.int32, (tokens, bins), 1)
    for side in range(2):
        values = part_ref[side] + other_ref[1 - side]
        goal = goal_ref[side]
        taken = lane == goal[:, 1:2].astype(jnp.int32)
        td_error = jnp.sum(jnp.where(taken, values, 0.0), axis=1, keepdims=True) - goal[:, :1]
        grad = grad_scale * jnp.where(taken, td_error, (CONSERVATIVE / (bins - 1)) * values)
        grad_ref[side * tokens : (side + 1) * tokens] = grad.astype(bf16)
        if side == 0:
            error_ref[...] = jnp.broadcast_to(td_error, error_ref.shape)
    out_ref[...] = jnp.dot(cols_ref[at], grad_ref[...], preferred_element_type=f32).astype(
        out_ref.dtype
    )


def term_kernel(offsets, cols_ref, grad_ref, *outs):
    for offset, out_ref in zip(offsets, outs):
        out_ref[...] = jnp.dot(
            cols_ref[offset], grad_ref[...], preferred_element_type=f32
        ).astype(out_ref.dtype)


def plain_body(features, online_head, target_head, action_bin, next_index, reward, terminal):
    tok_rows = features.shape[0]
    bin_count = online_head.shape[1]
    group_size = tok_rows * lax.axis_size("mp")
    all_tokens = group_size * lax.axis_size("dp")
    online_full = lax.all_gather(online_head, "dp", axis=0, tiled=True)
    columns = features
    target_logits = jnp.dot(
        columns,
        lax.all_gather(target_head, "dp", axis=0, tiled=True),
        preferred_element_type=jnp.float32,
    )
    best_value = jnp.max(target_logits, axis=1)
    local_next = next_index - lax.axis_index("dp") * group_size
    step_dim = jnp.arange(tok_rows, dtype=jnp.int32) % ADIM
    is_last = step_dim == ADIM - 1
    group_best = lax.all_gather(best_value, "mp", axis=0, tiled=True)
    next_best = jnp.take(group_best, local_next, axis=0)
    bootstrap = reward + DISCOUNT * (1.0 - terminal.astype(jnp.float32)) * next_best
    target_value = jnp.where(is_last, bootstrap, next_best)
    q_values = jnp.dot(features, online_full, preferred_element_type=jnp.float32)
    onehot = (jnp.arange(bin_count, dtype=jnp.int32)[None, :] == action_bin[:, None]).astype(
        jnp.float32
    )
    td_error = jnp.sum(q_values * onehot, axis=1) - target_value
    grad_scale = 1.0 / math.sqrt(all_tokens)
    q_grad = (
        grad_scale
        * (
            onehot * td_error[:, None]
            + (1.0 - onehot) * (CONSERVATIVE / (bin_count - 1)) * q_values
        )
    ).astype(jnp.bfloat16)
    columns = features
    grad_owned = lax.psum_scatter(
        lax.dot_general(
            columns, q_grad, (((0,), (0,)), ((), ())), preferred_element_type=jnp.float32
        ),
        "dp",
        scatter_dimension=0,
        tiled=True,
    )
    head_grad = lax.psum(grad_owned, "mp")
    return (td_error, head_grad)


def body(features, online_head, target_head, action_bin, next_index, reward, terminal):
    tokens = features.shape[0]
    head_rows, bins = online_head.shape
    mp_size = lax.axis_size("mp")
    dp_size = lax.axis_size("dp")
    odd = dp_size & (dp_size - 1) or mp_size & (mp_size - 1)
    if odd or head_rows % LANES or head_rows % (16 * mp_size):
        return plain_body(
            features, online_head, target_head, action_bin, next_index, reward, terminal
        )
    chips = dp_size // 2
    group_size = tokens * mp_size
    all_tokens = group_size * dp_size
    dp_at = lax.axis_index("dp")
    mp_at = lax.axis_index("mp")
    core, chip = dp_at & 1, dp_at >> 1

    offset = jnp.arange(chips, dtype=jnp.int32)
    owner = 2 * (chip ^ offset) + core
    sources = mp_at ^ jnp.arange(mp_size, dtype=jnp.int32)
    groups = (dp_at ^ jnp.arange(2, dtype=jnp.int32)) * group_size
    at = jnp.concatenate([owner, sources, groups])
    target_held = direct_hops(target_head, chips)
    theirs = across(features, 1)
    online_held = direct_hops(online_head, chips)

    scalars = jnp.stack(
        [
            action_bin.astype(f32),
            next_index.astype(f32),
            reward,
            terminal.astype(f32),
        ]
    )
    scalars = (scalars, across(scalars, 1))
    features, cols_turned = turned(at, features, theirs, chips, head_rows)

    last = chips - 1
    both = shape(2, tokens, bins)

    def logits(held):
        early = {o: p for o, p in held.items() if o < chips // 2}
        late = {o: p for o, p in held.items() if o not in early}
        part = partial_logits(head_rows, at, features, theirs, early)
        part = partial_logits(head_rows, at, features, theirs, late, part)
        return part, across(part, 1)

    parts = logits(target_held)
    lanes = -(-(tokens // ADIM) // LANES) * LANES
    best, firsts = call(best_kernel, (both, shape(2, lanes)), *parts)
    tables, mask = [firsts], 1
    while mask < mp_size:
        if mask > 1:
            out = shape(2 * mask, lanes)
            tables = [call(join_kernel, out, *tables)]
        tables.append(mixed(tables[0], mask))
        mask *= 2
    goal = call(
        functools.partial(goal_kernel, chips), both, at, best, *scalars, *tables, smem=1,
        scratch=[pltpu.VMEM((8, -(-tokens // LANES) * LANES), f32)],
    )

    parts = logits(online_held)
    grad_scale = 1.0 / math.sqrt(all_tokens)
    block = shape(head_rows, bins, dtype=bf16)
    q_grad, error, term = call(
        functools.partial(grad_kernel, grad_scale, last),
        (shape(2 * tokens, bins, dtype=bf16), shape(tokens, bins), block),
        *parts,
        goal,
        cols_turned,
    )
    arrived = [across(term, 2 * last)]
    rest = tuple(range(last - 1, 0, -1))
    *terms, owned = call(
        functools.partial(term_kernel, rest + (0,)),
        (*(block for _ in rest), shape(head_rows, bins)),
        cols_turned,
        q_grad,
    )
    arrived += [across(t, 2 * o) for o, t in zip(rest, terms)]
    for a in arrived:
        owned = owned + a.astype(f32)
    td_error = error[:, 0]

    rows = head_rows // mp_size

    def rows_of(k):
        return lax.dynamic_slice(owned, ((mp_at ^ k) * rows, 0), (rows, bins))

    order = sorted(range(1, mp_size), key=lambda k: -(k >> 1))
    piece = rows_of(0)
    for k in order:
        got = mixed(rows_of(k).astype(bf16), k)
        piece = piece + got.astype(f32)
    piece = piece.astype(bf16)
    head_grad = jnp.zeros((head_rows, bins), f32)
    for k in [0] + order:
        got = mixed(piece, k) if k else piece
        head_grad = lax.dynamic_update_slice(head_grad, got.astype(f32), ((mp_at ^ k) * rows, 0))
    return td_error, head_grad


def solution(mesh):
    placed = (
        P(("dp", "mp"), None),
        P("dp", None),
        P("dp", None),
        P(("dp", "mp")),
        P(("dp", "mp")),
        P(("dp", "mp")),
        P(("dp", "mp")),
    )


    return jax.shard_map(
        body,
        mesh=mesh,
        in_specs=placed,
        out_specs=(P(("dp", "mp")), P("dp", None)),
        check_vma=False,
    )
```
